256 devices in a mesh: seq: 64 (over x, z_hi, y), dp: 4 (over z_lo, core).
Axes of the slice: x: 4, y: 4, z: 8 (z_hi: 4, z_lo: 2; z = z_hi * 2 + z_lo), core: 2. Of those that a mesh axis runs over, the one named last changes fastest.
Arguments:
- tokens: bfloat16 [32768, 1024], P(('dp', 'seq')), parts along dimension 0, may hold values from -6 to 6
- norm_gain: float32 [1024], replicated, may hold values from 0.1 to 1.9
- filters: float32 [12, 8192], P(None, 'seq'), may hold values from -0.0625 to 0.0625
- mixing: bfloat16 [12, 1024, 1024], P(None, 'seq'), may hold values from -0.0546875 to 0.0546875
Outputs:
- mixed: bfloat16 [32768, 1024], P(('dp', 'seq')), parts along dimension 0
The draws below stay inside these ranges and needn't reach their ends.
There are 4 independent parts, one for each index of `dp`. The reference program is written for one: setup_inputs(seed, part) draws one part's arguments, and reference() takes and returns one part's arrays. A program takes and returns all parts, laid end to end along the dimension named above; an argument that names none is the same for every part. Nothing has to cross between parts.
All inputs are finite; a program needn't handle non-finite values.
Results may differ from the reference program's by a relative error of at most 0.0044.
Values may be sent and summed in bfloat16 or wider, within the bound.
A program may use at most 192 MiB of HBM per device.

```python
import jax
import jax.numpy as jnp
from jax import lax

D = 1024
K = 12
LENGTH = 8192


def block_levels(stream_key, dims, shards, least, high):
    def one(axis_at, parts):
        draws = jax.random.uniform(jax.random.fold_in(jax.random.fold_in(stream_key, 6), axis_at), (parts,), jnp.float32, least / len(shards), high / len(shards))
        return jnp.repeat(jnp.exp(draws), dims[axis_at] // parts).reshape((-1,) + (1,) * (len(dims) - axis_at - 1))

    gain = one(*shards[0])
    for cut in shards[1:]:
        gain = gain * one(*cut)
    return gain


def gaussian(key, dims, width, limit, shards=(), dtype=jnp.bfloat16):
    entries = jax.random.normal(key, dims, jnp.float32) * width
    if len(shards) > 0:
        entries = block_levels(key, dims, shards, -0.22, 0.18) * entries
    return jnp.clip(entries, min=-limit, max=limit).astype(dtype)


def setup_inputs(seed: int = 0, part: int = 0) -> dict:
    keys = jax.random.split(jax.random.key(seed), 5)
    part_splits = jax.random.split(jax.random.fold_in(keys[4], part), 5)
    tokens = gaussian(part_splits[0], (LENGTH, D), 1.0, 6.0, ((0, 64),))
    norm_gain = jnp.clip(1.0 + 0.18 * jax.random.normal(keys[1], (D,), jnp.float32), 0.1, 1.9)
    filters = gaussian(keys[2], (K, LENGTH), LENGTH ** -0.5, 0.0625, ((1, 64),), jnp.float32)
    mixing = gaussian(keys[3], (K, D, D), (K * D) ** -0.5, 0.0546875, ((1, 64),))
    return {"tokens": tokens, "norm_gain": norm_gain, "filters": filters, "mixing": mixing}


def reference(tokens, norm_gain, filters, mixing):
    values = tokens.astype(jnp.float32)
    scale_row = lax.rsqrt(lax.optimization_barrier(jnp.mean(values * values, axis=1, keepdims=True)) + 1e-05)
    normed = (values * scale_row * norm_gain).astype(jnp.bfloat16)
    total = 2 * LENGTH
    signal_hat = jnp.fft.rfft(normed.astype(jnp.float32), n=total, axis=0)
    filter_hat = jnp.fft.rfft(filters, n=total, axis=1)

    def one_filter(carry, inputs):
        spectrum, weight = inputs
        conv = jnp.fft.irfft(signal_hat * spectrum[:, None], n=total, axis=0)[:LENGTH]
        feats = conv.astype(jnp.bfloat16)
        return (carry + jnp.dot(feats, weight, preferred_element_type=jnp.float32), None)
    start = jnp.zeros((LENGTH, D), jnp.float32)
    branch, unused = lax.scan(one_filter, start, (filter_hat, mixing))
    return (values + branch).astype(jnp.bfloat16)
```

```python
import jax
import jax.numpy as jnp
from jax import lax
from jax.experimental import pallas as pl
from jax.experimental.pallas import tpu as pltpu
from jax.sharding import Mesh, PartitionSpec as P

AXES = ("x", "zh", "y", "zl", "q")
BLK = 128
NB = 64
GRP = 256
HALF = 6
PAD = 3


def remote(src, dst, send, recv, **where):
    return pltpu.make_async_remote_copy(
        src_ref=src,
        dst_ref=dst,
        send_sem=send,
        recv_sem=recv,
        device_id=where,
        device_id_type=pl.DeviceIdType.MESH,
    )


def kernel(
    tok_ref, gain_ref, filt_ref, mix_ref, out_ref,
    normed, taps, shifted, rolled, sig, acc, feats, weights, part_send, part_recv, part_own,
    red_send, red_recv, home_tok, fin,
    f_send, f_recv, n_send, n_recv, n_loc, t_send, t_recv, y_send, y_recv, z_send, z_recv,
    p_send, p_recv, wz_send, wz_recv, wy_send, wy_recv, w_loc, q_send, q_recv, x_send, x_recv,
    h_send, h_recv,
):
    x = lax.axis_index("x")
    zh = lax.axis_index("zh")
    y = lax.axis_index("y")
    zl = lax.axis_index("zl")
    q = lax.axis_index("q")
    me = (x * 4 + zh) * 4 + y
    to = {"zh": 2 * zl + q, "zl": zh % 2, "q": zh // 2}
    src = {"zh": 2 * q + zl, "zl": zh // 2, "q": zh % 2}
    own = jnp.logical_and(zh == 2 * zl + q, jnp.logical_and(zl == zh % 2, q == zh // 2))
    other = jnp.logical_not(own)
    idx_own = 8 * q + 4 * zl + y

    barrier = pltpu.get_barrier_semaphore()

    def greet(**where):
        pl.semaphore_signal(barrier, inc=1, device_id=where, device_id_type=pl.DeviceIdType.MESH)

    def greet_seq(d, carry):
        @pl.when(d != me)
        def _():
            greet(x=d // 16, zh=(d // 4) % 4, y=d % 4)

        return carry

    greet(q=1 - q)
    greet(zl=1 - zl)
    lax.fori_loop(0, NB, greet_seq, 0)
    for d in range(4):
        there = (x + d) % 4
        if d == 0:

            @pl.when(other)
            def _():
                greet(x=there, **to)
                greet(x=there, **src)
        else:
            greet(x=there, **to)
            greet(x=there, **src)

    values = tok_ref[...].astype(jnp.float32)
    scale_row = lax.rsqrt(jnp.mean(values * values, axis=1, keepdims=True) + 1e-05)
    normed[...] = (values * scale_row * gain_ref[...]).astype(jnp.bfloat16)
    taps[me] = filt_ref[q]

    pl.semaphore_wait(barrier, jnp.where(own, 71, 73).astype(jnp.int32))

    def first(d):
        to_x = (x + d) % 4
        return remote(
            normed.at[:, pl.ds(pl.multiple_of(GRP * to_x, GRP), GRP)],
            sig.at[x, 4 * zh + y],
            n_send.at[d],
            n_recv.at[d],
            x=to_x,
            **to,
        )

    def first_arrival(d):
        from_x = (x + 4 - d) % 4
        return remote(
            sig.at[from_x, idx_own], sig.at[from_x, idx_own], n_send.at[d], n_recv.at[d], x=from_x, **src
        )

    local_first = pltpu.make_async_copy(
        normed.at[:, pl.ds(pl.multiple_of(GRP * x, GRP), GRP)], sig.at[x, idx_own], n_loc.at[0]
    )
    tok_copy = remote(tok_ref, home_tok, t_send.at[0], t_recv.at[0], x=x, **to)
    local_tok = pltpu.make_async_copy(tok_ref, home_tok, n_loc.at[1])

    for d in range(1, 4):
        first(d).start()

    @pl.when(other)
    def _():
        first(0).start()

    @pl.when(own)
    def _():
        local_first.start()

    def tap_copy(d):
        return remote(
            filt_ref.at[q], taps.at[me], f_send.at[d], f_recv.at[me], x=d // 16, zh=(d // 4) % 4, y=d % 4
        )

    def tap_arrival(d):
        return remote(taps.at[d], taps.at[d], f_send.at[d], f_recv.at[d], x=d // 16, zh=(d // 4) % 4, y=d % 4)

    def send_taps(d, carry):
        @pl.when(d != me)
        def _():
            tap_copy(d).start()

        return carry

    lax.fori_loop(0, NB, send_taps, 0)

    mine = mix_ref.at[pl.ds(HALF * q, HALF)]

    def wz(e):
        return remote(mine, weights.at[:, 4 * zh + y], wz_send.at[e - 1], wz_recv.at[e - 1], zh=(zh + e) % 4)

    def wz_arrival(e):
        there = weights.at[:, 4 * ((zh + 4 - e) % 4) + y]
        return remote(there, there, wz_send.at[e - 1], wz_recv.at[e - 1], zh=(zh + e) % 4)

    def wy(e, d):
        held = weights.at[:, 4 * ((zh + 4 - e) % 4) + y]
        return remote(held, held, wy_send.at[e, d - 1], wy_recv.at[e, d - 1], y=(y + d) % 4)

    def wy_arrival(e, d):
        there = weights.at[:, 4 * ((zh + 4 - e) % 4) + (y + 4 - d) % 4]
        return remote(there, there, wy_send.at[e, d - 1], wy_recv.at[e, d - 1], y=(y + d) % 4)

    local_mix = pltpu.make_async_copy(mine, weights.at[:, 4 * zh + y], w_loc.at[0])
    local_mix.start()
    for e in range(1, 4):
        wz(e).start()

    @pl.when(other)
    def _():
        tok_copy.start()

    @pl.when(own)
    def _():
        local_tok.start()

    def shard(zl_src, d):
        return sig.at[:, 8 * q + 4 * zl_src + (y + 4 - d) % 4]

    def ycopy(d):
        return remote(shard(zl, 0), shard(zl, 0), y_send.at[d - 1], y_recv.at[d - 1], y=(y + d) % 4)

    def y_arrival(d):
        return remote(shard(zl, d), shard(zl, d), y_send.at[d - 1], y_recv.at[d - 1], y=(y + d) % 4)

    def zcopy(d):
        return remote(shard(zl, d), shard(zl, d), z_send.at[d], z_recv.at[d], zl=1 - zl)

    def z_arrival(d):
        return remote(shard(1 - zl, d), shard(1 - zl, d), z_send.at[d], z_recv.at[d], zl=1 - zl)

    def pcopy(far, d):
        held = shard(1 - zl if far else zl, d)
        return remote(held, held, p_send.at[4 * far + d], p_recv.at[4 * far + d], q=1 - q)

    def p_arrival(far, d):
        there = sig.at[:, 8 * (1 - q) + 4 * (1 - zl if far else zl) + (y + 4 - d) % 4]
        return remote(there, there, p_send.at[4 * far + d], p_recv.at[4 * far + d], q=1 - q)

    for d in range(1, 4):
        first_arrival(d).wait_recv()

    @pl.when(other)
    def _():
        first_arrival(0).wait_recv()

    @pl.when(own)
    def _():
        local_first.wait()

    for d in range(1, 4):
        ycopy(d).start()
    zcopy(0).start()
    pcopy(0, 0).start()

    def wait_taps(d, carry):
        @pl.when(d != me)
        def _():
            tap_arrival(d).wait_recv()

        return carry

    lax.fori_loop(0, NB, wait_taps, 0)

    rolled[...] = jnp.zeros_like(rolled)
    shifted[:, NB * BLK :] = jnp.zeros((HALF * BLK, PAD * BLK), jnp.bfloat16)
    causal = lax.broadcasted_iota(jnp.int32, (BLK, BLK), 1) <= lax.broadcasted_iota(jnp.int32, (BLK, BLK), 0)

    def build(m, carry):
        lanes = pl.ds(pl.multiple_of(BLK * (NB - 1 - m), BLK), BLK)
        for k in range(HALF):
            rows = slice(BLK * k, BLK * (k + 1))
            line = jnp.broadcast_to(taps[m, k : k + 1, :], (BLK, BLK))
            now = pltpu.roll(line, 1, 1, stride=1, stride_axis=0)
            shifted[rows, lanes] = jnp.where(causal, now, rolled[rows, :]).astype(jnp.bfloat16)
            rolled[rows, :] = now
        return carry

    lax.fori_loop(0, NB, build, 0)

    for d in range(1, 4):
        y_arrival(d).wait_recv()
        zcopy(d).start()
        pcopy(0, d).start()
    local_mix.wait()
    for d in range(1, 4):
        wy(0, d).start()
    for d in range(4):
        z_arrival(d).wait_recv()
        pcopy(1, d).start()
    for e in range(1, 4):
        wz_arrival(e).wait_recv()
        for d in range(1, 4):
            wy(e, d).start()
    for d in range(4):
        p_arrival(0, d).wait_recv()
        p_arrival(1, d).wait_recv()

    def conv(slot):
        which = jnp.where(slot < 4, 1 - q, q)
        i = 16 * (slot % 4) + 8 * which + 4 * zl + y
        first_lane = BLK * (NB - 1 - i)
        acc[...] = jnp.zeros_like(acc)

        def chunk(c, carry):
            lhs = shifted[:, pl.ds(pl.multiple_of(first_lane + 4 * BLK * c, BLK), 4 * BLK)]
            rhs = sig[c // 4, pl.ds(4 * (c % 4), 4)].reshape(4 * BLK, GRP)
            acc[...] += jnp.dot(lhs, rhs, preferred_element_type=jnp.float32)
            return carry

        lax.fori_loop(0, (i + 4) // 4, chunk, 0)
        for k in range(HALF):
            feats[pl.ds(pl.multiple_of(BLK * slot, BLK), BLK), GRP * k : GRP * (k + 1)] = acc[
                BLK * k : BLK * (k + 1), :
            ].astype(jnp.bfloat16)

    def project(base, n):
        rows = feats[base : base + 4 * BLK, :]
        cols = pl.ds(pl.multiple_of(256 * n, 256), 256)
        return cols, jnp.dot(
            rows, weights[:, :, :, cols].reshape(HALF * GRP, 256), preferred_element_type=jnp.float32
        )

    def conv_step(slot, carry):
        conv(slot)
        return carry

    lax.fori_loop(0, 4, conv_step, 0)

    for e in range(4):
        for d in range(1, 4):
            wy_arrival(e, d).wait_recv()

    def project_send(n, carry):
        cols, value = project(0, n)
        part_send[:, cols] = value.astype(jnp.bfloat16)
        return carry

    lax.fori_loop(0, 4, project_send, 0)
    swap = remote(part_send, part_recv, q_send.at[0], q_recv.at[0], q=1 - q)
    swap.start()

    lax.fori_loop(4, 8, conv_step, 0)

    swap.wait_recv()

    def project_own(n, carry):
        cols, value = project(4 * BLK, n)
        total = value + part_recv[:, cols].astype(jnp.float32)
        part_own[:, cols] = total
        red_send[:, cols] = total.astype(jnp.bfloat16)
        return carry

    lax.fori_loop(0, 4, project_own, 0)

    def red(d):
        there = (x + d) % 4
        return remote(
            red_send.at[pl.ds(pl.multiple_of(BLK * there, BLK), BLK)],
            red_recv.at[d - 1],
            x_send.at[d - 1],
            x_recv.at[d - 1],
            x=there,
        )

    for d in range(1, 4):
        red(d).start()

    @pl.when(other)
    def _():
        tok_copy.wait_recv()

    @pl.when(own)
    def _():
        local_tok.wait()

    for d in range(1, 4):
        red(d).wait_recv()
    total = part_own[pl.ds(pl.multiple_of(BLK * x, BLK), BLK), :]
    for d in range(1, 4):
        total = total + red_recv[d - 1].astype(jnp.float32)
    fin[...] = (home_tok[...].astype(jnp.float32) + total).astype(jnp.bfloat16)

    back = remote(fin, out_ref, h_send.at[0], h_recv.at[0], x=x, **src)
    local_back = pltpu.make_async_copy(fin, out_ref, n_loc.at[2])

    @pl.when(other)
    def _():
        back.start()

    @pl.when(own)
    def _():
        local_back.start()
        local_back.wait()

    for d in range(1, 4):
        first(d).wait_send()
        ycopy(d).wait_send()
        wz(d).wait_send()
        red(d).wait_send()
        for e in range(4):
            wy(e, d).wait_send()
    for d in range(4):
        zcopy(d).wait_send()
        pcopy(0, d).wait_send()
        pcopy(1, d).wait_send()
    swap.wait_send()

    def wait_sent(d, carry):
        @pl.when(d != me)
        def _():
            tap_copy(d).wait_send()

        return carry

    lax.fori_loop(0, NB, wait_sent, 0)

    @pl.when(other)
    def _():
        first(0).wait_send()
        tok_copy.wait_send()
        back.wait_send()
        back.wait_recv()


def local(tokens, norm_gain, filters, mixing):
    rows, width = tokens.shape
    count = filters.shape[0]
    flipped = jnp.flip(filters, axis=1).reshape(2, count // 2, BLK)
    flipped = jnp.pad(flipped, ((0, 0), (0, 8 - count // 2), (0, 0)))
    bf16, f32 = jnp.bfloat16, jnp.float32
    dma = pltpu.SemaphoreType.DMA
    vmem = pl.BlockSpec(memory_space=pltpu.VMEM)
    return pl.pallas_call(
        kernel,
        out_shape=jax.ShapeDtypeStruct((rows, width), bf16),
        in_specs=[vmem] * 4,
        out_specs=vmem,
        scratch_shapes=[
            pltpu.VMEM((rows, width), bf16),
            pltpu.VMEM((NB, 8, BLK), f32),
            pltpu.VMEM((HALF * BLK, (NB + PAD) * BLK), bf16),
            pltpu.VMEM((HALF * BLK, BLK), f32),
            pltpu.VMEM((4, 16, BLK, GRP), bf16),
            pltpu.VMEM((HALF * BLK, GRP), f32),
            pltpu.VMEM((8 * BLK, HALF * GRP), bf16),
            pltpu.VMEM((HALF, 16, 16, width), bf16),
            pltpu.VMEM((4 * BLK, width), bf16),
            pltpu.VMEM((4 * BLK, width), bf16),
            pltpu.VMEM((4 * BLK, width), f32),
            pltpu.VMEM((4 * BLK, width), bf16),
            pltpu.VMEM((3, BLK, width), bf16),
            pltpu.VMEM((rows, width), bf16),
            pltpu.VMEM((rows, width), bf16),
            dma((NB,)), dma((NB,)), dma((4,)), dma((4,)), dma((3,)), dma((1,)), dma((1,)),
            dma((3,)), dma((3,)), dma((4,)), dma((4,)), dma((8,)), dma((8,)),
            dma((3,)), dma((3,)), dma((4, 3)), dma((4, 3)), dma((1,)), dma((1,)), dma((1,)),
            dma((3,)), dma((3,)), dma((1,)), dma((1,)),
        ],
        compiler_params=pltpu.CompilerParams(
            collective_id=0, has_side_effects=True, vmem_limit_bytes=56 * 1024 * 1024
        ),
    )(tokens, norm_gain.reshape(1, width), flipped, mixing)


def solution(mesh):
    grid = Mesh(mesh.devices.reshape(4, 4, 4, 2, 2), AXES)
    seq = ("x", "zh", "y")
    in_specs = (P(("zl", "q") + seq, None), P(), P(None, seq), P(None, seq, None))
    out_specs = P(("zl", "q") + seq, None)
    return jax.shard_map(local, mesh=grid, in_specs=in_specs, out_specs=out_specs, check_vma=False)
```

```python
import jax
import jax.numpy as jnp
from jax import lax
from jax.experimental import pallas as pl
from jax.experimental.pallas import tpu as pltpu
from jax.sharding import Mesh, PartitionSpec as P

AXES = ("x", "zh", "y", "zl", "q")
BLK = 128
NB = 64
GRP = 256
HALF = 6
PAD = 3
PIECE = 32
AROUND = [(a, b, c) for a in range(4) for b in range(4) for c in range(4) if a + b + c > 0]
ROWS = 384


def remote(src, dst, send, recv, **where):
    return pltpu.make_async_remote_copy(
        src_ref=src,
        dst_ref=dst,
        send_sem=send,
        recv_sem=recv,
        device_id=where,
        device_id_type=pl.DeviceIdType.MESH,
    )


def kernel(
    tok_ref, gain_ref, filt_ref, mix_ref, out_ref,
    normed, tap_own, taps, shifted, rolled, sig, acc, feats, weights, part_send, part_recv, part_own,
    red_send, red_recv, home_tok, fin,
    f_send, f_recv, n_send, n_recv, n_loc, t_send, t_recv, y_send, y_recv, z_send, z_recv,
    p_send, p_recv, wz_send, wz_recv, wy_send, wy_recv, w_loc, q_send, q_recv, x_send, x_recv,
    h_send, h_recv, h_loc,
):
    x = lax.axis_index("x")
    zh = lax.axis_index("zh")
    y = lax.axis_index("y")
    zl = lax.axis_index("zl")
    q = lax.axis_index("q")
    me = (x * 4 + zh) * 4 + y
    to = {"zh": 2 * zl + q, "zl": zh % 2, "q": zh // 2}
    src = {"zh": 2 * q + zl, "zl": zh // 2, "q": zh % 2}
    own = jnp.logical_and(zh == 2 * zl + q, jnp.logical_and(zl == zh % 2, q == zh // 2))
    other = jnp.logical_not(own)
    idx_own = 8 * q + 4 * zl + y
    xs = [(x + d) % 4 for d in range(4)]
    zhs = [(zh + d) % 4 for d in range(4)]
    ys = [(y + d) % 4 for d in range(4)]

    barrier = pltpu.get_barrier_semaphore()

    def greet(**where):
        pl.semaphore_signal(barrier, inc=1, device_id=where, device_id_type=pl.DeviceIdType.MESH)

    greet(q=1 - q)
    greet(zl=1 - zl)
    for dx, dz, dy in AROUND:
        greet(x=xs[dx], zh=zhs[dz], y=ys[dy])
    for d in range(4):
        there = (x + d) % 4
        if d == 0:

            @pl.when(other)
            def _():
                greet(x=there, **to)
                greet(x=there, **src)
        else:
            greet(x=there, **to)
            greet(x=there, **src)

    values = tok_ref[...].astype(jnp.float32)
    scale_row = lax.rsqrt(jnp.mean(values * values, axis=1, keepdims=True) + 1e-05)
    normed[...] = (values * scale_row * gain_ref[...]).astype(jnp.bfloat16)
    pick = lax.broadcasted_iota(jnp.int32, (8, 2 * HALF), 1) == lax.broadcasted_iota(jnp.int32, (8, 2 * HALF), 0) + HALF * q
    pick = jnp.logical_and(pick, lax.broadcasted_iota(jnp.int32, (8, 2 * HALF), 0) < HALF)
    turn = lax.broadcasted_iota(jnp.int32, (BLK, BLK), 0) + lax.broadcasted_iota(jnp.int32, (BLK, BLK), 1) == BLK - 1
    half = jnp.dot(pick.astype(jnp.bfloat16), filt_ref[...].astype(jnp.bfloat16), preferred_element_type=jnp.float32)
    half = jnp.dot(half.astype(jnp.bfloat16), turn.astype(jnp.bfloat16), preferred_element_type=jnp.float32)
    tap_own[...] = half.astype(jnp.bfloat16)
    taps[me] = half.astype(jnp.bfloat16)

    pl.semaphore_wait(barrier, jnp.where(own, 71, 73).astype(jnp.int32))

    def first(d):
        to_x = (x + d) % 4
        return remote(
            normed.at[:, pl.ds(pl.multiple_of(GRP * to_x, GRP), GRP)],
            sig.at[x, 4 * zh + y],
            n_send.at[d],
            n_recv.at[d],
            x=to_x,
            **to,
        )

    def first_arrival(d):
        from_x = (x + 4 - d) % 4
        return remote(
            sig.at[from_x, idx_own], sig.at[from_x, idx_own], n_send.at[d], n_recv.at[d], x=from_x, **src
        )

    local_first = pltpu.make_async_copy(
        normed.at[:, pl.ds(pl.multiple_of(GRP * x, GRP), GRP)], sig.at[x, idx_own], n_loc.at[0]
    )
    def tok_copy(d):
        to_x = (x + d) % 4
        return remote(
            tok_ref.at[pl.ds(pl.multiple_of(PIECE * to_x, PIECE), PIECE)],
            home_tok.at[x],
            t_send.at[d],
            t_recv.at[d],
            x=to_x,
            **to,
        )

    def tok_arrival(d):
        from_x = (x + 4 - d) % 4
        return remote(home_tok.at[from_x], home_tok.at[from_x], t_send.at[d], t_recv.at[d], x=from_x, **src)

    local_tok = pltpu.make_async_copy(
        tok_ref.at[pl.ds(pl.multiple_of(PIECE * x, PIECE), PIECE)], home_tok.at[x], n_loc.at[1]
    )

    for d in range(1, 4):
        first(d).start()

    @pl.when(other)
    def _():
        first(0).start()

    @pl.when(own)
    def _():
        local_first.start()

    for dx, dz, dy in AROUND:
        remote(tap_own, taps.at[me], f_send.at[0], f_recv.at[0], x=xs[dx], zh=zhs[dz], y=ys[dy]).start()
    all_taps = remote(taps.at[: NB - 1], taps.at[: NB - 1], f_send.at[0], f_recv.at[0], x=xs[1])

    mine = mix_ref.at[pl.ds(HALF * q, HALF)]

    def wz(e):
        return remote(mine, weights.at[:, 4 * zh + y], wz_send.at[e - 1], wz_recv.at[e - 1], zh=(zh + e) % 4)

    def wz_arrival(e):
        there = weights.at[:, 4 * ((zh + 4 - e) % 4) + y]
        return remote(there, there, wz_send.at[e - 1], wz_recv.at[e - 1], zh=(zh + e) % 4)

    def wy(e, d):
        held = weights.at[:, 4 * zhs[-e % 4] + y]
        return remote(held, held, wy_send.at[e, d - 1], wy_recv.at[e, d - 1], y=ys[d])

    def wy_arrival(e, d):
        there = weights.at[:, 4 * zhs[-e % 4] + ys[4 - d]]
        return remote(there, there, wy_send.at[e, d - 1], wy_recv.at[e, d - 1], y=ys[d])

    def wr(e, r, d):
        held = weights.at[3 * r : 3 * r + 3, 4 * zhs[-e % 4] + ys[4 - d]]
        return remote(held, held, wy_send.at[e, 1 + 2 * r], wy_recv.at[e, 1 + 2 * r], y=ys[1 + 2 * r])

    def relay_weights(e):
        for r in range(2):
            wy_arrival(e, 1 + 2 * r).wait_recv()
            wr(e, r, 1 + 2 * r).start()

    def wy_own(d):
        return remote(mine, weights.at[:, 4 * zh + y], wy_send.at[0, d - 1], wy_recv.at[0, d - 1], y=(y + d) % 4)

    local_mix = pltpu.make_async_copy(mine, weights.at[:, 4 * zh + y], w_loc.at[0])
    local_mix.start()
    for d in (1, 3):
        wy_own(d).start()
    def shard(zl_src, d, h):
        return sig.at[2 * h : 2 * h + 2, 8 * q + 4 * zl_src + (y + 4 - d) % 4]

    def along(kind, zl_src, h, d, back=0):
        there = shard(zl_src, back, h)
        return remote(there, there, y_send.at[4 * kind + d - 1], y_recv.at[4 * kind + d - 1], y=ys[d])

    def passed(kind, zl_src, h, r, back):
        there = sig.at[2 * h + r : 2 * h + r + 1, 8 * q + 4 * zl_src + ys[4 - back]]
        return remote(there, there, y_send.at[4 * kind + 1 + 2 * r], y_recv.at[4 * kind + 1 + 2 * r], y=ys[1 + 2 * r])

    kinds = {"a": (0, zl, 1), "b": (1, zl, 0), "z": (2, 1 - zl, 0)}

    def ystart(name):
        for d in (1, 3):
            along(*kinds[name], d).start()

    def ynear(name, r):
        along(*kinds[name], 1 + 2 * r, 1 + 2 * r).wait_recv()
        passed(*kinds[name], r, 1 + 2 * r).start()

    def yfar(name):
        for r in range(2):
            passed(*kinds[name], r, 2).wait_recv()

    def zpre(zl_src):
        return remote(shard(zl_src, 0, 0), shard(zl_src, 0, 0), z_send.at[4], z_recv.at[4], zl=1 - zl)

    def za(d, zl_src):
        return remote(shard(zl_src, d, 1), shard(zl_src, d, 1), z_send.at[d], z_recv.at[d], zl=1 - zl)

    def both(n, zl_src, d, h, qq):
        held = sig.at[2 * h : 2 * h + 2, 8 * qq + 4 * zl_src + (y + 4 - d) % 4]
        return remote(held, held, p_send.at[n], p_recv.at[n], q=1 - q)

    def pieces(h, qq):
        return [both(8 * h + 4 * far + d, 1 - zl if far else zl, d, h, qq) for far in range(2) for d in range(4)]

    give = [pieces(h, q) for h in range(2)]
    take = [pieces(h, 1 - q) for h in range(2)]

    for d in range(1, 4):
        first_arrival(d).wait_recv()

    @pl.when(other)
    def _():
        first_arrival(0).wait_recv()

    @pl.when(own)
    def _():
        local_first.wait()

    zpre(zl).start()
    za(0, zl).start()
    ystart("a")
    ystart("b")
    give[0][0].start()
    give[1][0].start()
    local_mix.wait()
    relay_weights(0)
    zpre(1 - zl).wait_recv()
    ystart("z")
    give[0][4].start()

    all_taps.wait_recv()
    rolled[...] = jnp.zeros_like(rolled)
    shifted[:, NB * BLK :] = jnp.zeros((HALF * BLK, PAD * BLK), jnp.bfloat16)
    causal = lax.broadcasted_iota(jnp.int32, (BLK, BLK), 1) <= lax.broadcasted_iota(jnp.int32, (BLK, BLK), 0)

    def build(m, carry):
        lanes = pl.ds(pl.multiple_of(BLK * (NB - 1 - m), BLK), BLK)
        chunk = taps[m].astype(jnp.float32)
        for k in range(HALF):
            rows = slice(BLK * k, BLK * (k + 1))
            line = jnp.broadcast_to(chunk[k : k + 1, :], (BLK, BLK))
            now = pltpu.roll(line, 1, 1, stride=1, stride_axis=0)
            shifted[rows, lanes] = jnp.where(causal, now, rolled[rows, :]).astype(jnp.bfloat16)
            rolled[rows, :] = now
        return carry

    def build_some(n):
        lax.fori_loop(NB // 4 * n, NB // 4 * (n + 1), build, 0, unroll=2)

    build_some(0)
    for r in range(2):
        ynear("a", r)
        za(1 + 2 * r, zl).start()
        give[1][1 + 2 * r].start()
    for r in range(2):
        ynear("b", r)
        give[0][1 + 2 * r].start()
    for e in (1, 3, 2):
        wz(e).start()
    build_some(1)
    yfar("a")
    za(2, zl).start()
    give[1][2].start()
    for r in range(2):
        ynear("z", r)
        give[0][5 + 2 * r].start()
    build_some(2)
    yfar("b")
    give[0][2].start()
    build_some(3)
    yfar("z")
    give[0][6].start()
    all_taps.wait_send()
    for piece in take[0]:
        piece.wait_recv()

    def conv(xh, mine_too):
        j = 2 * xh + (q if mine_too else 1 - q)
        first_lane = BLK * (NB - 1 - (8 * j + 4 * zl + y))
        base = 2 * BLK * xh + (BLK if mine_too else 0)
        acc[...] = jnp.zeros_like(acc)

        def add(start, count):
            lanes = pl.ds(pl.multiple_of(first_lane + BLK * start, BLK), count * BLK)
            rhs = sig[start // 16, pl.ds(start % 16, count)].reshape(count * BLK, GRP)
            for r in range(0, HALF * BLK, ROWS):
                acc[r : r + ROWS, :] += jnp.dot(
                    shifted[r : r + ROWS, lanes], rhs, preferred_element_type=jnp.float32
                )

        def chunk(c, carry):
            add(8 * c, 8)
            return carry

        def tail(c, carry):
            add(8 * j + 4 * c, 4)
            return carry

        lax.fori_loop(0, j, chunk, 0)
        lax.fori_loop(0, 1 + zl, tail, 0)
        for k in range(HALF):
            feats[pl.ds(pl.multiple_of(base, BLK), BLK), GRP * k : GRP * (k + 1)] = acc[BLK * k : BLK * (k + 1), :].astype(
                jnp.bfloat16
            )

    def conv_pair(xh, carry):
        conv(xh, False)
        conv(xh, True)
        return carry

    def conv_one(xh, mine_too):
        def step(n, carry):
            conv(n, mine_too)
            return carry

        lax.fori_loop(xh, xh + 1, step, 0)

    lax.fori_loop(0, 1, conv_pair, 0)
    for e in (1, 3):
        wz_arrival(e).wait_recv()
        for d in (1, 3):
            wy(e, d).start()
    lax.fori_loop(1, 2, conv_pair, 0)
    for d in (0, 1, 3, 2):
        za(d, 1 - zl).wait_recv()
        give[1][4 + d].start()
    for d in range(1, 4):
        tok_copy(d).start()

    @pl.when(other)
    def _():
        tok_copy(0).start()

    @pl.when(own)
    def _():
        local_tok.start()

    for d in range(1, 4):
        first(d).wait_send()
    wz_arrival(2).wait_recv()
    for d in (1, 3):
        wy(2, d).start()
    relay_weights(1)
    relay_weights(3)
    for piece in take[1]:
        piece.wait_recv()
    lax.fori_loop(2, 3, conv_pair, 0)
    relay_weights(2)
    conv_one(3, False)
    for e in range(4):
        for r in range(2):
            wr(e, r, 2).wait_recv()

    def swap(xh):
        return remote(part_send.at[xh], part_recv.at[xh], q_send.at[xh], q_recv.at[xh], q=1 - q)

    def project(xh):
        rows = feats[2 * BLK * xh : 2 * BLK * (xh + 1), :]

        def tile(n, carry):
            cols = pl.ds(pl.multiple_of(256 * n, 256), 256)
            value = jnp.dot(
                rows, weights[:, :, :, cols].reshape(HALF * GRP, 256), preferred_element_type=jnp.float32
            )
            part_send[xh, :, cols] = value[:BLK].astype(jnp.bfloat16)
            part_own[xh, :, cols] = value[BLK:]
            return carry

        lax.fori_loop(0, 4, tile, 0)
        swap(xh).start()

    def red(xh, d):
        there = (x + d) % 4
        return remote(
            red_send.at[xh, pl.ds(pl.multiple_of(PIECE * there, PIECE), PIECE)],
            red_recv.at[xh, d - 1],
            x_send.at[xh, d - 1],
            x_recv.at[xh, d - 1],
            x=there,
        )

    def merge(xh):
        swap(xh).wait_recv()
        total = part_own[xh] + part_recv[xh].astype(jnp.float32)
        part_own[xh] = total
        red_send[xh] = total.astype(jnp.bfloat16)
        for d in range(1, 4):
            red(xh, d).start()

    def back(xh):
        return remote(
            fin.at[xh],
            out_ref.at[pl.ds(pl.multiple_of(PIECE * x, PIECE), PIECE)],
            h_send.at[xh],
            h_recv.at[x],
            x=xh,
            **src,
        )

    def back_arrival(xw):
        there = out_ref.at[PIECE * xw : PIECE * (xw + 1)]
        return remote(there, there, h_send.at[xw], h_recv.at[xw], x=xw, **to)

    local_back = pltpu.make_async_copy(
        fin.at[x], out_ref.at[pl.ds(pl.multiple_of(PIECE * x, PIECE), PIECE)], h_loc.at[0]
    )

    def finish(xh):
        for d in range(1, 4):
            red(xh, d).wait_recv()
        total = part_own[xh, pl.ds(pl.multiple_of(PIECE * x, PIECE), PIECE), :]
        for d in range(1, 4):
            total = total + red_recv[xh, d - 1].astype(jnp.float32)
        fin[xh] = (home_tok[xh].astype(jnp.float32) + total).astype(jnp.bfloat16)
        here = jnp.logical_and(own, x == xh)

        @pl.when(jnp.logical_not(here))
        def _():
            back(xh).start()

        @pl.when(here)
        def _():
            local_back.start()

    project(0)
    project(1)
    merge(0)
    project(2)
    merge(1)
    conv_one(3, True)
    merge(2)
    project(3)
    for d in range(1, 4):
        tok_arrival(d).wait_recv()

    @pl.when(other)
    def _():
        tok_arrival(0).wait_recv()

    @pl.when(own)
    def _():
        local_tok.wait()

    finish(0)
    merge(3)
    for xh in range(1, 4):
        finish(xh)

    for xw in range(4):
        here = jnp.logical_and(own, x == xw)

        @pl.when(jnp.logical_not(here))
        def _():
            back_arrival(xw).wait_recv()
            back(xw).wait_send()

        @pl.when(here)
        def _():
            local_back.wait()

    for d in range(1, 4):
        tok_copy(d).wait_send()
        wz(d).wait_send()
        for xh in range(4):
            red(xh, d).wait_send()
    for r in range(2):
        for name in kinds:
            along(*kinds[name], 1 + 2 * r).wait_send()
            passed(*kinds[name], r, 1 + 2 * r).wait_send()
        wy_own(1 + 2 * r).wait_send()
        for e in range(4):
            wr(e, r, 1 + 2 * r).wait_send()
            if e > 0:
                wy(e, 1 + 2 * r).wait_send()
    zpre(zl).wait_send()
    for d in range(4):
        za(d, zl).wait_send()
        swap(d).wait_send()
    for piece in give[0] + give[1]:
        piece.wait_send()

    @pl.when(other)
    def _():
        first(0).wait_send()
        tok_copy(0).wait_send()


def local(tokens, norm_gain, filters, mixing):
    rows, width = tokens.shape
    bf16, f32 = jnp.bfloat16, jnp.float32
    dma = pltpu.SemaphoreType.DMA
    vmem = pl.BlockSpec(memory_space=pltpu.VMEM)
    return pl.pallas_call(
        kernel,
        out_shape=jax.ShapeDtypeStruct((rows, width), bf16),
        in_specs=[vmem] * 4,
        out_specs=vmem,
        scratch_shapes=[
            pltpu.VMEM((rows, width), bf16),
            pltpu.VMEM((8, BLK), bf16),
            pltpu.VMEM((NB, 8, BLK), bf16),
            pltpu.VMEM((HALF * BLK, (NB + PAD) * BLK), bf16),
            pltpu.VMEM((HALF * BLK, BLK), f32),
            pltpu.VMEM((4, 16, BLK, GRP), bf16),
            pltpu.VMEM((HALF * BLK, GRP), f32),
            pltpu.VMEM((8 * BLK, HALF * GRP), bf16),
            pltpu.VMEM((HALF, 16, 16, width), bf16),
            pltpu.VMEM((4, BLK, width), bf16),
            pltpu.VMEM((4, BLK, width), bf16),
            pltpu.VMEM((4, BLK, width), f32),
            pltpu.VMEM((4, BLK, width), bf16),
            pltpu.VMEM((4, 3, PIECE, width), bf16),
            pltpu.VMEM((4, PIECE, width), bf16),
            pltpu.VMEM((4, PIECE, width), bf16),
            dma((1,)), dma((1,)), dma((4,)), dma((4,)), dma((2,)), dma((4,)), dma((4,)),
            dma((12,)), dma((12,)), dma((5,)), dma((5,)), dma((16,)), dma((16,)),
            dma((3,)), dma((3,)), dma((4, 4)), dma((4, 4)), dma((1,)), dma((4,)), dma((4,)),
            dma((4, 3)), dma((4, 3)), dma((4,)), dma((4,)), dma((1,)),
        ],
        compiler_params=pltpu.CompilerParams(
            collective_id=0, has_side_effects=True, vmem_limit_bytes=56 * 1024 * 1024
        ),
    )(tokens, norm_gain.reshape(1, width), filters, mixing)


def solution(mesh):
    grid = Mesh(mesh.devices.reshape(4, 4, 4, 2, 2), AXES)
    seq = ("x", "zh", "y")
    in_specs = (P(("zl", "q") + seq, None), P(), P(None, seq), P(None, seq, None))
    out_specs = P(("zl", "q") + seq, None)
    return jax.shard_map(local, mesh=grid, in_specs=in_specs, out_specs=out_specs, check_vma=False)
```

```python
import jax
import jax.numpy as jnp
from jax import lax
from jax.experimental import pallas as pl
from jax.experimental.pallas import tpu as pltpu
from jax.sharding import Mesh, PartitionSpec as P

AXES = ("x", "zh", "y", "zl", "q")
BLK = 128
NB = 64
GRP = 256
HALF = 6
PAD = 3
PIECE = 32
AROUND = [(a, 0, c) for a in range(4) for c in range(4) if a + c > 0] + [(0, b, 0) for b in range(1, 4)]
ROWS = 384


def remote(src, dst, send, recv, **where):
    return pltpu.make_async_remote_copy(
        src_ref=src,
        dst_ref=dst,
        send_sem=send,
        recv_sem=recv,
        device_id=where,
        device_id_type=pl.DeviceIdType.MESH,
    )


def kernel(
    tok_ref, gain_ref, filt_ref, mix_ref, out_ref,
    normed, tap_own, taps, shifted, rolled, sig, acc, feats, weights, part_send, part_recv, part_own,
    red_send, red_recv, home_tok, fin,
    f_send, f_recv, n_send, n_recv, n_loc, t_send, t_recv, y_send, y_recv, z_send, z_recv,
    p_send, p_recv, wz_send, wz_recv, wy_send, wy_recv, w_loc, q_send, q_recv, x_send, x_recv,
    h_send, h_recv, h_loc,
):
    x = lax.axis_index("x")
    zh = lax.axis_index("zh")
    y = lax.axis_index("y")
    zl = lax.axis_index("zl")
    q = lax.axis_index("q")
    me = (x * 4 + zh) * 4 + y
    to = {"zh": 2 * zl + q, "zl": zh % 2, "q": zh // 2}
    src = {"zh": 2 * q + zl, "zl": zh // 2, "q": zh % 2}
    own = jnp.logical_and(zh == 2 * zl + q, jnp.logical_and(zl == zh % 2, q == zh // 2))
    other = jnp.logical_not(own)
    idx_own = 8 * q + 4 * zl + y
    xs = [(x + d) % 4 for d in range(4)]
    zhs = [(zh + d) % 4 for d in range(4)]
    ys = [(y + d) % 4 for d in range(4)]

    barrier = pltpu.get_barrier_semaphore()

    def greet(**where):
        pl.semaphore_signal(barrier, inc=1, device_id=where, device_id_type=pl.DeviceIdType.MESH)

    greet(q=1 - q)
    greet(zl=1 - zl)
    for dx, dz, dy in AROUND:
        greet(x=xs[dx], zh=zhs[dz], y=ys[dy])
    for d in range(4):
        there = (x + d) % 4
        if d == 0:

            @pl.when(other)
            def _():
                greet(x=there, **to)
                greet(x=there, **src)
        else:
            greet(x=there, **to)
            greet(x=there, **src)

    values = tok_ref[...].astype(jnp.float32)
    scale_row = lax.rsqrt(jnp.mean(values * values, axis=1, keepdims=True) + 1e-05)
    normed[...] = (values * scale_row * gain_ref[...]).astype(jnp.bfloat16)
    pick = lax.broadcasted_iota(jnp.int32, (8, 2 * HALF), 1) == lax.broadcasted_iota(jnp.int32, (8, 2 * HALF), 0) + HALF * q
    pick = jnp.logical_and(pick, lax.broadcasted_iota(jnp.int32, (8, 2 * HALF), 0) < HALF)
    turn = lax.broadcasted_iota(jnp.int32, (BLK, BLK), 0) + lax.broadcasted_iota(jnp.int32, (BLK, BLK), 1) == BLK - 1
    half = jnp.dot(pick.astype(jnp.bfloat16), filt_ref[...].astype(jnp.bfloat16), preferred_element_type=jnp.float32)
    half = jnp.dot(half.astype(jnp.bfloat16), turn.astype(jnp.bfloat16), preferred_element_type=jnp.float32)
    tap_own[...] = half.astype(jnp.bfloat16)
    slot_own = 16 * x + 4 * y + zh
    taps[slot_own] = half.astype(jnp.bfloat16)

    pl.semaphore_wait(barrier, jnp.where(own, 26, 28).astype(jnp.int32))

    def first(d):
        to_x = (x + d) % 4
        return remote(
            normed.at[:, pl.ds(pl.multiple_of(GRP * to_x, GRP), GRP)],
            sig.at[x, 4 * zh + y],
            n_send.at[d],
            n_recv.at[d],
            x=to_x,
            **to,
        )

    def first_arrival(d):
        from_x = (x + 4 - d) % 4
        return remote(
            sig.at[from_x, idx_own], sig.at[from_x, idx_own], n_send.at[d], n_recv.at[d], x=from_x, **src
        )

    local_first = pltpu.make_async_copy(
        normed.at[:, pl.ds(pl.multiple_of(GRP * x, GRP), GRP)], sig.at[x, idx_own], n_loc.at[0]
    )
    def tok_copy(d):
        to_x = (x + d) % 4
        return remote(
            tok_ref.at[pl.ds(pl.multiple_of(PIECE * to_x, PIECE), PIECE)],
            home_tok.at[x],
            t_send.at[d],
            t_recv.at[d],
            x=to_x,
            **to,
        )

    def tok_arrival(d):
        from_x = (x + 4 - d) % 4
        return remote(home_tok.at[from_x], home_tok.at[from_x], t_send.at[d], t_recv.at[d], x=from_x, **src)

    local_tok = pltpu.make_async_copy(
        tok_ref.at[pl.ds(pl.multiple_of(PIECE * x, PIECE), PIECE)], home_tok.at[x], n_loc.at[1]
    )

    for d in range(1, 4):
        remote(tap_own, taps.at[slot_own], f_send.at[0], f_recv.at[0], zh=zhs[d]).start()
    near_taps = remote(taps.at[:3], taps.at[:3], f_send.at[0], f_recv.at[0], zh=zhs[1])
    all_taps = remote(taps.at[:60], taps.at[:60], f_send.at[1], f_recv.at[1], x=xs[1])
    column = taps.at[pl.ds(pl.multiple_of(16 * x + 4 * y, 4), 4)]

    for d in range(1, 4):
        first(d).start()

    @pl.when(other)
    def _():
        first(0).start()

    @pl.when(own)
    def _():
        local_first.start()

    mine = mix_ref.at[pl.ds(HALF * q, HALF)]

    def wz(e):
        return remote(mine, weights.at[:, 4 * zh + y], wz_send.at[e - 1], wz_recv.at[e - 1], zh=(zh + e) % 4)

    def wz_arrival(e):
        there = weights.at[:, 4 * ((zh + 4 - e) % 4) + y]
        return remote(there, there, wz_send.at[e - 1], wz_recv.at[e - 1], zh=(zh + e) % 4)

    def wy(e, d):
        held = weights.at[:, 4 * zhs[-e % 4] + y]
        return remote(held, held, wy_send.at[e, d - 1], wy_recv.at[e, d - 1], y=ys[d])

    def wy_arrival(e, d):
        there = weights.at[:, 4 * zhs[-e % 4] + ys[4 - d]]
        return remote(there, there, wy_send.at[e, d - 1], wy_recv.at[e, d - 1], y=ys[d])

    def wr(e, r, d):
        held = weights.at[3 * r : 3 * r + 3, 4 * zhs[-e % 4] + ys[4 - d]]
        return remote(held, held, wy_send.at[e, 1 + 2 * r], wy_recv.at[e, 1 + 2 * r], y=ys[1 + 2 * r])

    def relay_weights(e):
        for r in range(2):
            wy_arrival(e, 1 + 2 * r).wait_recv()
            wr(e, r, 1 + 2 * r).start()

    def wy_own(d):
        return remote(mine, weights.at[:, 4 * zh + y], wy_send.at[0, d - 1], wy_recv.at[0, d - 1], y=(y + d) % 4)

    local_mix = pltpu.make_async_copy(mine, weights.at[:, 4 * zh + y], w_loc.at[0])
    local_mix.start()
    for d in (1, 3):
        wy_own(d).start()
    def shard(zl_src, d, h):
        return sig.at[2 * h : 2 * h + 2, 8 * q + 4 * zl_src + (y + 4 - d) % 4]

    def along(kind, zl_src, h, d, back=0):
        there = shard(zl_src, back, h)
        return remote(there, there, y_send.at[4 * kind + d - 1], y_recv.at[4 * kind + d - 1], y=ys[d])

    def passed(kind, zl_src, h, r, back):
        there = sig.at[2 * h + r : 2 * h + r + 1, 8 * q + 4 * zl_src + ys[4 - back]]
        return remote(there, there, y_send.at[4 * kind + 1 + 2 * r], y_recv.at[4 * kind + 1 + 2 * r], y=ys[1 + 2 * r])

    kinds = {"b0": (0, zl, 0), "z0": (1, 1 - zl, 0), "b1": (2, zl, 1), "z1": (3, 1 - zl, 1)}

    def ystart(name):
        for d in (1, 3):
            along(*kinds[name], d).start()

    def ynear(name):
        for r in range(2):
            along(*kinds[name], 1 + 2 * r, 1 + 2 * r).wait_recv()
            passed(*kinds[name], r, 1 + 2 * r).start()
        for d in (1, 3):
            give[int(name[1])][d + (4 if name[0] == "z" else 0)].start()

    def yfar(name):
        for r in range(2):
            passed(*kinds[name], r, 2).wait_recv()
        give[int(name[1])][2 + (4 if name[0] == "z" else 0)].start()

    def zpre(zl_src, h):
        return remote(shard(zl_src, 0, h), shard(zl_src, 0, h), z_send.at[h], z_recv.at[h], zl=1 - zl)

    def both(n, zl_src, d, h, qq):
        held = sig.at[2 * h : 2 * h + 2, 8 * qq + 4 * zl_src + (y + 4 - d) % 4]
        return remote(held, held, p_send.at[n], p_recv.at[n], q=1 - q)

    def pieces(h, qq):
        return [both(8 * h + 4 * far + d, 1 - zl if far else zl, d, h, qq) for far in range(2) for d in range(4)]

    give = [pieces(h, q) for h in range(2)]
    take = [pieces(h, 1 - q) for h in range(2)]

    rolled[...] = jnp.zeros_like(rolled)
    shifted[:, NB * BLK :] = jnp.zeros((HALF * BLK, PAD * BLK), jnp.bfloat16)
    causal = lax.broadcasted_iota(jnp.int32, (BLK, BLK), 1) <= lax.broadcasted_iota(jnp.int32, (BLK, BLK), 0)

    def build(m, carry):
        lanes = pl.ds(pl.multiple_of(BLK * (NB - 1 - m), BLK), BLK)
        chunk = taps[16 * (m // 16) + 4 * (m % 4) + (m // 4) % 4].astype(jnp.float32)
        for k in range(HALF):
            rows = slice(BLK * k, BLK * (k + 1))
            line = jnp.broadcast_to(chunk[k : k + 1, :], (BLK, BLK))
            now = pltpu.roll(line, 1, 1, stride=1, stride_axis=0)
            shifted[rows, lanes] = jnp.where(causal, now, rolled[rows, :]).astype(jnp.bfloat16)
            rolled[rows, :] = now
        return carry

    def build_some(n):
        lax.fori_loop(NB // 4 * n, NB // 4 * (n + 1), build, 0, unroll=2)

    near_taps.wait_recv()
    for dx in range(4):
        for dy in range(4):
            if dx + dy > 0:
                remote(column, column, f_send.at[1], f_recv.at[1], x=xs[dx], y=ys[dy]).start()
    all_taps.wait_recv()
    for d in range(1, 4):
        first_arrival(d).wait_recv()

    @pl.when(other)
    def _():
        first_arrival(0).wait_recv()

    @pl.when(own)
    def _():
        local_first.wait()

    zpre(zl, 0).start()
    ystart("b0")
    zpre(zl, 1).start()
    give[0][0].start()
    give[1][0].start()
    build_some(0)
    zpre(1 - zl, 0).wait_recv()
    ystart("z0")
    give[0][4].start()
    for e in (1, 3, 2):
        wz(e).start()
    build_some(1)
    build_some(2)
    ynear("b0")
    build_some(3)
    ynear("z0")
    ystart("b1")
    zpre(1 - zl, 1).wait_recv()
    give[1][4].start()
    ystart("z1")
    local_mix.wait()
    relay_weights(0)
    yfar("b0")
    yfar("z0")
    near_taps.wait_send()
    all_taps.wait_send()
    for piece in take[0]:
        piece.wait_recv()

    def conv(xh, mine_too):
        j = 2 * xh + jnp.where(mine_too == 1, q, 1 - q)
        first_lane = BLK * (NB - 1 - (8 * j + 4 * zl + y))
        base = BLK * (2 * xh + mine_too)
        acc[...] = jnp.zeros_like(acc)

        def add(start, count, rows):
            lanes = pl.ds(pl.multiple_of(first_lane + BLK * start, BLK), count * BLK)
            if count == 16:
                rhs = sig[start // 16].reshape(count * BLK, GRP)
            else:
                rhs = sig[start // 16, pl.ds(start % 16, count)].reshape(count * BLK, GRP)
            for r in range(0, HALF * BLK, rows):
                acc[r : r + rows, :] += jnp.dot(
                    shifted[r : r + rows, lanes], rhs, preferred_element_type=jnp.float32
                )

        def long(c, carry):
            add(16 * c, 16, 256)
            return carry

        def chunk(c, carry):
            add(16 * (j // 2) + 8 * c, 8, ROWS)
            return carry

        def tail(c, carry):
            add(8 * j + 4 * c, 4, ROWS)
            return carry

        lax.fori_loop(0, j // 2, long, 0)
        lax.fori_loop(0, j % 2 + zl, chunk, 0)

        @pl.when(zl == 0)
        def _():
            tail(0, 0)

        for k in range(HALF):
            feats[pl.ds(pl.multiple_of(base, BLK), BLK), GRP * k : GRP * (k + 1)] = acc[BLK * k : BLK * (k + 1), :].astype(
                jnp.bfloat16
            )

    def conv_some(xh, start, stop):
        def step(n, carry):
            conv(xh, n)
            return carry

        lax.fori_loop(start, stop, step, 0)

    def conv_pair(xh):
        conv_some(xh, 0, 2)

    conv_pair(0)
    ynear("b1")
    ynear("z1")
    for e in (1, 3):
        wz_arrival(e).wait_recv()
        for d in (1, 3):
            wy(e, d).start()
    conv_pair(1)
    yfar("b1")
    yfar("z1")
    wz_arrival(2).wait_recv()
    for d in (1, 3):
        wy(2, d).start()
    for d in range(1, 4):
        tok_copy(d).start()

    @pl.when(other)
    def _():
        tok_copy(0).start()

    @pl.when(own)
    def _():
        local_tok.start()

    for d in range(1, 4):
        first(d).wait_send()
    for piece in take[1]:
        piece.wait_recv()
    conv_pair(2)
    relay_weights(1)
    relay_weights(3)
    conv_some(3, 0, 1)
    relay_weights(2)
    for e in range(4):
        for r in range(2):
            wr(e, r, 2).wait_recv()

    def swap(xh):
        return remote(part_send.at[xh], part_recv.at[xh], q_send.at[xh], q_recv.at[xh], q=1 - q)

    def project(xh):
        rows = feats[2 * BLK * xh : 2 * BLK * (xh + 1), :]

        def tile(n, carry):
            cols = pl.ds(pl.multiple_of(256 * n, 256), 256)
            value = jnp.dot(
                rows, weights[:, :, :, cols].reshape(HALF * GRP, 256), preferred_element_type=jnp.float32
            )
            part_send[xh, :, cols] = value[:BLK].astype(jnp.bfloat16)
            part_own[xh, :, cols] = value[BLK:]
            return carry

        lax.fori_loop(0, 4, tile, 0)
        swap(xh).start()

    def red(xh, d):
        there = (x + d) % 4
        return remote(
            red_send.at[xh, pl.ds(pl.multiple_of(PIECE * there, PIECE), PIECE)],
            red_recv.at[xh, d - 1],
            x_send.at[xh, d - 1],
            x_recv.at[xh, d - 1],
            x=there,
        )

    def merge(xh):
        swap(xh).wait_recv()
        total = part_own[xh] + part_recv[xh].astype(jnp.float32)
        part_own[xh] = total
        red_send[xh] = total.astype(jnp.bfloat16)
        for d in range(1, 4):
            red(xh, d).start()

    def back(xh):
        return remote(
            fin.at[xh],
            out_ref.at[pl.ds(pl.multiple_of(PIECE * x, PIECE), PIECE)],
            h_send.at[xh],
            h_recv.at[x],
            x=xh,
            **src,
        )

    def back_arrival(xw):
        there = out_ref.at[PIECE * xw : PIECE * (xw + 1)]
        return remote(there, there, h_send.at[xw], h_recv.at[xw], x=xw, **to)

    local_back = pltpu.make_async_copy(
        fin.at[x], out_ref.at[pl.ds(pl.multiple_of(PIECE * x, PIECE), PIECE)], h_loc.at[0]
    )

    def finish(xh):
        for d in range(1, 4):
            red(xh, d).wait_recv()
        total = part_own[xh, pl.ds(pl.multiple_of(PIECE * x, PIECE), PIECE), :]
        for d in range(1, 4):
            total = total + red_recv[xh, d - 1].astype(jnp.float32)
        fin[xh] = (home_tok[xh].astype(jnp.float32) + total).astype(jnp.bfloat16)
        here = jnp.logical_and(own, x == xh)

        @pl.when(jnp.logical_not(here))
        def _():
            back(xh).start()

        @pl.when(here)
        def _():
            local_back.start()

    project(0)
    project(1)
    merge(0)
    project(2)
    merge(1)
    conv_some(3, 1, 2)
    merge(2)
    project(3)
    for d in range(1, 4):
        tok_arrival(d).wait_recv()

    @pl.when(other)
    def _():
        tok_arrival(0).wait_recv()

    @pl.when(own)
    def _():
        local_tok.wait()

    merge(3)
    for xh in range(4):
        finish(xh)

    for xw in range(4):
        here = jnp.logical_and(own, x == xw)

        @pl.when(jnp.logical_not(here))
        def _():
            back_arrival(xw).wait_recv()
            back(xw).wait_send()

        @pl.when(here)
        def _():
            local_back.wait()

    for d in range(1, 4):
        tok_copy(d).wait_send()
        wz(d).wait_send()
        for xh in range(4):
            red(xh, d).wait_send()
    for r in range(2):
        for name in kinds:
            along(*kinds[name], 1 + 2 * r).wait_send()
            passed(*kinds[name], r, 1 + 2 * r).wait_send()
        wy_own(1 + 2 * r).wait_send()
        for e in range(4):
            wr(e, r, 1 + 2 * r).wait_send()
            if e > 0:
                wy(e, 1 + 2 * r).wait_send()
    for h in range(2):
        zpre(zl, h).wait_send()
    for d in range(4):
        swap(d).wait_send()
    for piece in give[0] + give[1]:
        piece.wait_send()

    @pl.when(other)
    def _():
        first(0).wait_send()
        tok_copy(0).wait_send()


def local(tokens, norm_gain, filters, mixing):
    rows, width = tokens.shape
    bf16, f32 = jnp.bfloat16, jnp.float32
    dma = pltpu.SemaphoreType.DMA
    vmem = pl.BlockSpec(memory_space=pltpu.VMEM)
    result = pl.BlockSpec(memory_space=pl.ANY)
    return pl.pallas_call(
        kernel,
        out_shape=jax.ShapeDtypeStruct((rows, width), bf16),
        in_specs=[vmem] * 4,
        out_specs=result,
        scratch_shapes=[
            pltpu.VMEM((rows, width), bf16),
            pltpu.VMEM((8, BLK), bf16),
            pltpu.VMEM((NB, 8, BLK), bf16),
            pltpu.VMEM((HALF * BLK, (NB + PAD) * BLK), bf16),
            pltpu.VMEM((HALF * BLK, BLK), f32),
            pltpu.VMEM((4, 16, BLK, GRP), bf16),
            pltpu.VMEM((HALF * BLK, GRP), f32),
            pltpu.VMEM((8 * BLK, HALF * GRP), bf16),
            pltpu.VMEM((HALF, 16, 16, width), bf16),
            pltpu.VMEM((4, BLK, width), bf16),
            pltpu.VMEM((4, BLK, width), bf16),
            pltpu.VMEM((4, BLK, width), f32),
            pltpu.VMEM((4, BLK, width), bf16),
            pltpu.VMEM((4, 3, PIECE, width), bf16),
            pltpu.VMEM((4, PIECE, width), bf16),
            pltpu.VMEM((4, PIECE, width), bf16),
            dma((2,)), dma((2,)), dma((4,)), dma((4,)), dma((2,)), dma((4,)), dma((4,)),
            dma((16,)), dma((16,)), dma((2,)), dma((2,)), dma((16,)), dma((16,)),
            dma((3,)), dma((3,)), dma((4, 4)), dma((4, 4)), dma((1,)), dma((4,)), dma((4,)),
            dma((4, 3)), dma((4, 3)), dma((4,)), dma((4,)), dma((1,)),
        ],
        compiler_params=pltpu.CompilerParams(
            collective_id=0, has_side_effects=True, vmem_limit_bytes=56 * 1024 * 1024
        ),
    )(tokens, norm_gain.reshape(1, width), filters, mixing)


def solution(mesh):
    grid = Mesh(mesh.devices.reshape(4, 4, 4, 2, 2), AXES)
    seq = ("x", "zh", "y")
    in_specs = (P(("zl", "q") + seq, None), P(), P(None, seq), P(None, seq, None))
    out_specs = P(("zl", "q") + seq, None)
    return jax.shard_map(local, mesh=grid, in_specs=in_specs, out_specs=out_specs, check_vma=False)
```

```python
import jax
import jax.numpy as jnp
from jax import lax
from jax.experimental import pallas as pl
from jax.experimental.pallas import tpu as pltpu
from jax.sharding import Mesh, PartitionSpec as P

AXES = ("x", "zh", "y", "zl", "q")
BLK = 128
NB = 64
GRP = 256
HALF = 6
PAD = 3
PIECE = 32
AROUND = [(a, 0, c) for a in range(4) for c in range(4) if a + c > 0] + [(0, b, 0) for b in range(1, 4)]
ROWS = 384


def remote(src, dst, send, recv, **where):
    return pltpu.make_async_remote_copy(
        src_ref=src,
        dst_ref=dst,
        send_sem=send,
        recv_sem=recv,
        device_id=where,
        device_id_type=pl.DeviceIdType.MESH,
    )


def kernel(
    tok_ref, gain_ref, filt_ref, mix_ref, out_ref,
    normed, tap_own, taps, shifted, rolled, sig, acc, feats, weights, part_send, part_recv, part_own,
    red_send, red_recv, home_tok, fin,
    f_send, f_recv, n_send, n_recv, n_loc, t_send, t_recv, y_send, y_recv, z_send, z_recv,
    p_send, p_recv, wz_send, wz_recv, wy_send, wy_recv, w_loc, q_send, q_recv, x_send, x_recv,
    h_send, h_recv, h_loc,
):
    x = lax.axis_index("x")
    zh = lax.axis_index("zh")
    y = lax.axis_index("y")
    zl = lax.axis_index("zl")
    q = lax.axis_index("q")
    me = (x * 4 + zh) * 4 + y
    to = {"zh": 2 * zl + q, "zl": zh % 2, "q": zh // 2}
    src = {"zh": 2 * q + zl, "zl": zh // 2, "q": zh % 2}
    own = jnp.logical_and(zh == 2 * zl + q, jnp.logical_and(zl == zh % 2, q == zh // 2))
    other = jnp.logical_not(own)
    idx_own = 8 * q + 4 * zl + y
    xs = [(x + d) % 4 for d in range(4)]
    zhs = [(zh + d) % 4 for d in range(4)]
    ys = [(y + d) % 4 for d in range(4)]

    barrier = pltpu.get_barrier_semaphore()

    def greet(**where):
        pl.semaphore_signal(barrier, inc=1, device_id=where, device_id_type=pl.DeviceIdType.MESH)

    greet(q=1 - q)
    greet(zl=1 - zl)
    for dx, dz, dy in AROUND:
        greet(x=xs[dx], zh=zhs[dz], y=ys[dy])
    for d in range(4):
        there = (x + d) % 4
        if d == 0:

            @pl.when(other)
            def _():
                greet(x=there, **to)
                greet(x=there, **src)
        else:
            greet(x=there, **to)
            greet(x=there, **src)

    values = tok_ref[...].astype(jnp.float32)
    scale_row = lax.rsqrt(jnp.mean(values * values, axis=1, keepdims=True) + 1e-05)
    normed[...] = (values * scale_row * gain_ref[...]).astype(jnp.bfloat16)
    pick = lax.broadcasted_iota(jnp.int32, (8, 2 * HALF), 1) == lax.broadcasted_iota(jnp.int32, (8, 2 * HALF), 0) + HALF * q
    pick = jnp.logical_and(pick, lax.broadcasted_iota(jnp.int32, (8, 2 * HALF), 0) < HALF)
    turn = lax.broadcasted_iota(jnp.int32, (BLK, BLK), 0) + lax.broadcasted_iota(jnp.int32, (BLK, BLK), 1) == BLK - 1
    half = jnp.dot(pick.astype(jnp.bfloat16), filt_ref[...].astype(jnp.bfloat16), preferred_element_type=jnp.float32)
    half = jnp.dot(half.astype(jnp.bfloat16), turn.astype(jnp.bfloat16), preferred_element_type=jnp.float32)
    tap_own[...] = half.astype(jnp.bfloat16)
    slot_own = 16 * x + 4 * y + zh
    taps[slot_own] = half.astype(jnp.bfloat16)

    pl.semaphore_wait(barrier, jnp.where(own, 26, 28).astype(jnp.int32))

    def first(d):
        to_x = (x + d) % 4
        return remote(
            normed.at[:, pl.ds(pl.multiple_of(GRP * to_x, GRP), GRP)],
            sig.at[x, 4 * zh + y],
            n_send.at[d],
            n_recv.at[d],
            x=to_x,
            **to,
        )

    def first_arrival(d):
        from_x = (x + 4 - d) % 4
        return remote(
            sig.at[from_x, idx_own], sig.at[from_x, idx_own], n_send.at[d], n_recv.at[d], x=from_x, **src
        )

    local_first = pltpu.make_async_copy(
        normed.at[:, pl.ds(pl.multiple_of(GRP * x, GRP), GRP)], sig.at[x, idx_own], n_loc.at[0]
    )
    def tok_copy(d):
        to_x = (x + d) % 4
        return remote(
            tok_ref.at[pl.ds(pl.multiple_of(PIECE * to_x, PIECE), PIECE)],
            home_tok.at[x],
            t_send.at[d],
            t_recv.at[d],
            x=to_x,
            **to,
        )

    def tok_arrival(d):
        from_x = (x + 4 - d) % 4
        return remote(home_tok.at[from_x], home_tok.at[from_x], t_send.at[d], t_recv.at[d], x=from_x, **src)

    local_tok = pltpu.make_async_copy(
        tok_ref.at[pl.ds(pl.multiple_of(PIECE * x, PIECE), PIECE)], home_tok.at[x], n_loc.at[1]
    )

    for d in range(1, 4):
        remote(tap_own, taps.at[slot_own], f_send.at[0], f_recv.at[0], zh=zhs[d]).start()
    near_taps = remote(taps.at[:3], taps.at[:3], f_send.at[0], f_recv.at[0], zh=zhs[1])
    all_taps = remote(taps.at[:60], taps.at[:60], f_send.at[1], f_recv.at[1], x=xs[1])
    column = taps.at[pl.ds(pl.multiple_of(16 * x + 4 * y, 4), 4)]

    for d in range(1, 4):
        first(d).start()

    @pl.when(other)
    def _():
        first(0).start()

    @pl.when(own)
    def _():
        local_first.start()

    mine = mix_ref.at[pl.ds(HALF * q, HALF)]

    def wz(e):
        return remote(mine, weights.at[:, 4 * zh + y], wz_send.at[e - 1], wz_recv.at[e - 1], zh=(zh + e) % 4)

    def wz_arrival(e):
        there = weights.at[:, 4 * ((zh + 4 - e) % 4) + y]
        return remote(there, there, wz_send.at[e - 1], wz_recv.at[e - 1], zh=(zh + e) % 4)

    def wy(e, d):
        held = weights.at[:, 4 * zhs[-e % 4] + y]
        return remote(held, held, wy_send.at[e, d - 1], wy_recv.at[e, d - 1], y=ys[d])

    def wy_arrival(e, d):
        there = weights.at[:, 4 * zhs[-e % 4] + ys[4 - d]]
        return remote(there, there, wy_send.at[e, d - 1], wy_recv.at[e, d - 1], y=ys[d])

    def wr(e, r, d):
        held = weights.at[3 * r : 3 * r + 3, 4 * zhs[-e % 4] + ys[4 - d]]
        return remote(held, held, wy_send.at[e, 1 + 2 * r], wy_recv.at[e, 1 + 2 * r], y=ys[1 + 2 * r])

    def relay_weights(e):
        for r in range(2):
            wy_arrival(e, 1 + 2 * r).wait_recv()
            wr(e, r, 1 + 2 * r).start()

    def wy_own(d):
        return remote(mine, weights.at[:, 4 * zh + y], wy_send.at[0, d - 1], wy_recv.at[0, d - 1], y=(y + d) % 4)

    local_mix = pltpu.make_async_copy(mine, weights.at[:, 4 * zh + y], w_loc.at[0])
    local_mix.start()
    for d in (1, 3):
        wy_own(d).start()
    def shard(zl_src, d, h):
        return sig.at[2 * h : 2 * h + 2, 8 * q + 4 * zl_src + (y + 4 - d) % 4]

    def along(kind, zl_src, h, d, back=0):
        there = shard(zl_src, back, h)
        return remote(there, there, y_send.at[4 * kind + d - 1], y_recv.at[4 * kind + d - 1], y=ys[d])

    def passed(kind, zl_src, h, r, back):
        there = sig.at[2 * h + r : 2 * h + r + 1, 8 * q + 4 * zl_src + ys[4 - back]]
        return remote(there, there, y_send.at[4 * kind + 1 + 2 * r], y_recv.at[4 * kind + 1 + 2 * r], y=ys[1 + 2 * r])

    kinds = {"b0": (0, zl, 0), "z0": (1, 1 - zl, 0), "b1": (2, zl, 1), "z1": (3, 1 - zl, 1)}

    def ystart(name):
        for d in (1, 3):
            along(*kinds[name], d).start()

    def ynear(name):
        for r in range(2):
            along(*kinds[name], 1 + 2 * r, 1 + 2 * r).wait_recv()
            passed(*kinds[name], r, 1 + 2 * r).start()
        for d in (1, 3):
            give[int(name[1])][d + (4 if name[0] == "z" else 0)].start()

    def yfar(name):
        for r in range(2):
            passed(*kinds[name], r, 2).wait_recv()
        give[int(name[1])][2 + (4 if name[0] == "z" else 0)].start()

    def zpre(zl_src, h):
        return remote(shard(zl_src, 0, h), shard(zl_src, 0, h), z_send.at[h], z_recv.at[h], zl=1 - zl)

    def both(n, zl_src, d, h, qq):
        held = sig.at[2 * h : 2 * h + 2, 8 * qq + 4 * zl_src + (y + 4 - d) % 4]
        return remote(held, held, p_send.at[n], p_recv.at[n], q=1 - q)

    def pieces(h, qq):
        return [both(8 * h + 4 * far + d, 1 - zl if far else zl, d, h, qq) for far in range(2) for d in range(4)]

    give = [pieces(h, q) for h in range(2)]
    take = [pieces(h, 1 - q) for h in range(2)]

    rolled[...] = jnp.zeros_like(rolled)
    shifted[:, NB * BLK :] = jnp.zeros((HALF * BLK, PAD * BLK), jnp.bfloat16)
    causal = lax.broadcasted_iota(jnp.int32, (BLK, BLK), 1) <= lax.broadcasted_iota(jnp.int32, (BLK, BLK), 0)

    def build(m, carry):
        lanes = pl.ds(pl.multiple_of(BLK * (NB - 1 - m), BLK), BLK)
        chunk = taps[16 * (m // 16) + 4 * (m % 4) + (m // 4) % 4].astype(jnp.float32)
        for k in range(HALF):
            rows = slice(BLK * k, BLK * (k + 1))
            line = jnp.broadcast_to(chunk[k : k + 1, :], (BLK, BLK))
            now = pltpu.roll(line, 1, 1, stride=1, stride_axis=0)
            shifted[rows, lanes] = jnp.where(causal, now, rolled[rows, :]).astype(jnp.bfloat16)
            rolled[rows, :] = now
        return carry

    def build_some(n):
        lax.fori_loop(NB // 4 * n, NB // 4 * (n + 1), build, 0, unroll=2)

    near_taps.wait_recv()
    for dx in range(4):
        for dy in range(4):
            if dx + dy > 0:
                remote(column, column, f_send.at[1], f_recv.at[1], x=xs[dx], y=ys[dy]).start()
    all_taps.wait_recv()
    for d in range(1, 4):
        first_arrival(d).wait_recv()

    @pl.when(other)
    def _():
        first_arrival(0).wait_recv()

    @pl.when(own)
    def _():
        local_first.wait()

    zpre(zl, 0).start()
    ystart("b0")
    zpre(zl, 1).start()
    give[0][0].start()
    give[1][0].start()
    build_some(0)
    zpre(1 - zl, 0).wait_recv()
    ystart("z0")
    give[0][4].start()
    for e in (1, 3, 2):
        wz(e).start()
    build_some(1)
    build_some(2)
    ynear("b0")
    build_some(3)
    ynear("z0")
    ystart("b1")
    zpre(1 - zl, 1).wait_recv()
    give[1][4].start()
    ystart("z1")
    local_mix.wait()
    relay_weights(0)
    yfar("b0")
    yfar("z0")
    near_taps.wait_send()
    all_taps.wait_send()
    for piece in take[0]:
        piece.wait_recv()

    def conv(xh, mine_too):
        j = 2 * xh + jnp.where(mine_too == 1, q, 1 - q)
        first_lane = BLK * (NB - 1 - (8 * j + 4 * zl + y))
        base = BLK * (2 * xh + mine_too)
        acc[...] = jnp.zeros_like(acc)

        def add(start, count, rows):
            lanes = pl.ds(pl.multiple_of(first_lane + BLK * start, BLK), count * BLK)
            if count == 16:
                rhs = sig[start // 16].reshape(count * BLK, GRP)
            else:
                rhs = sig[start // 16, pl.ds(start % 16, count)].reshape(count * BLK, GRP)
            for r in range(0, HALF * BLK, rows):
                acc[r : r + rows, :] += jnp.dot(
                    shifted[r : r + rows, lanes], rhs, preferred_element_type=jnp.float32
                )

        def long(c, carry):
            add(16 * c, 16, 256)
            return carry

        def chunk(c, carry):
            add(16 * (j // 2) + 8 * c, 8, ROWS)
            return carry

        def tail(c, carry):
            add(8 * j + 4 * c, 4, ROWS)
            return carry

        lax.fori_loop(0, j // 2, long, 0)
        lax.fori_loop(0, j % 2 + zl, chunk, 0)

        @pl.when(zl == 0)
        def _():
            tail(0, 0)

        for k in range(HALF):
            feats[pl.ds(pl.multiple_of(base, BLK), BLK), GRP * k : GRP * (k + 1)] = acc[BLK * k : BLK * (k + 1), :].astype(
                jnp.bfloat16
            )

    def conv_some(xh, start, stop):
        def step(n, carry):
            conv(xh, n)
            return carry

        lax.fori_loop(start, stop, step, 0)

    def conv_pair(xh):
        conv_some(xh, 0, 2)

    conv_pair(0)
    ynear("b1")
    ynear("z1")
    for e in (1, 3):
        wz_arrival(e).wait_recv()
        for d in (1, 3):
            wy(e, d).start()
    conv_pair(1)
    yfar("b1")
    yfar("z1")
    wz_arrival(2).wait_recv()
    for d in (1, 3):
        wy(2, d).start()
    for d in range(1, 4):
        tok_copy(d).start()

    @pl.when(other)
    def _():
        tok_copy(0).start()

    @pl.when(own)
    def _():
        local_tok.start()

    for d in range(1, 4):
        first(d).wait_send()
    for piece in take[1]:
        piece.wait_recv()
    conv_pair(2)
    relay_weights(1)
    relay_weights(3)
    conv_some(3, 0, 1)
    relay_weights(2)
    for e in range(4):
        for r in range(2):
            wr(e, r, 2).wait_recv()

    def swap(xh):
        return remote(part_send.at[xh], part_recv.at[xh], q_send.at[xh], q_recv.at[xh], q=1 - q)

    def project(xh):
        rows = feats[2 * BLK * xh : 2 * BLK * (xh + 1), :]

        def tile(n, carry):
            cols = pl.ds(pl.multiple_of(256 * n, 256), 256)
            value = jnp.dot(
                rows, weights[:, :, :, cols].reshape(HALF * GRP, 256), preferred_element_type=jnp.float32
            )
            part_send[xh, :, cols] = value[:BLK].astype(jnp.bfloat16)
            part_own[xh, :, cols] = value[BLK:]
            return carry

        lax.fori_loop(0, 4, tile, 0)
        swap(xh).start()

    def red(xh, d):
        there = (x + d) % 4
        return remote(
            red_send.at[xh, pl.ds(pl.multiple_of(PIECE * there, PIECE), PIECE)],
            red_recv.at[xh, d - 1],
            x_send.at[xh, d - 1],
            x_recv.at[xh, d - 1],
            x=there,
        )

    def merge(xh):
        swap(xh).wait_recv()
        total = part_own[xh] + part_recv[xh].astype(jnp.float32)
        part_own[xh] = total
        red_send[xh] = total.astype(jnp.bfloat16)
        for d in range(1, 4):
            red(xh, d).start()

    def back(xh):
        return remote(
            fin.at[xh],
            out_ref.at[pl.ds(pl.multiple_of(PIECE * x, PIECE), PIECE)],
            h_send.at[xh],
            h_recv.at[x],
            x=xh,
            **src,
        )

    def back_arrival(xw):
        there = out_ref.at[PIECE * xw : PIECE * (xw + 1)]
        return remote(there, there, h_send.at[xw], h_recv.at[xw], x=xw, **to)

    local_back = pltpu.make_async_copy(
        fin.at[x], out_ref.at[pl.ds(pl.multiple_of(PIECE * x, PIECE), PIECE)], h_loc.at[0]
    )

    def finish(xh):
        for d in range(1, 4):
            red(xh, d).wait_recv()
        total = part_own[xh, pl.ds(pl.multiple_of(PIECE * x, PIECE), PIECE), :]
        for d in range(1, 4):
            total = total + red_recv[xh, d - 1].astype(jnp.float32)
        fin[xh] = (home_tok[xh].astype(jnp.float32) + total).astype(jnp.bfloat16)
        here = jnp.logical_and(own, x == xh)

        @pl.when(jnp.logical_not(here))
        def _():
            back(xh).start()

        @pl.when(here)
        def _():
            local_back.start()

    project(0)
    project(1)
    merge(0)
    project(2)
    merge(1)
    merge(2)
    conv_some(3, 1, 2)
    project(3)
    for d in range(1, 4):
        tok_arrival(d).wait_recv()

    @pl.when(other)
    def _():
        tok_arrival(0).wait_recv()

    @pl.when(own)
    def _():
        local_tok.wait()

    merge(3)
    for xh in range(4):
        finish(xh)

    for xw in range(4):
        here = jnp.logical_and(own, x == xw)

        @pl.when(jnp.logical_not(here))
        def _():
            back_arrival(xw).wait_recv()
            back(xw).wait_send()

        @pl.when(here)
        def _():
            local_back.wait()

    for d in range(1, 4):
        tok_copy(d).wait_send()
        wz(d).wait_send()
        for xh in range(4):
            red(xh, d).wait_send()
    for r in range(2):
        for name in kinds:
            along(*kinds[name], 1 + 2 * r).wait_send()
            passed(*kinds[name], r, 1 + 2 * r).wait_send()
        wy_own(1 + 2 * r).wait_send()
        for e in range(4):
            wr(e, r, 1 + 2 * r).wait_send()
            if e > 0:
                wy(e, 1 + 2 * r).wait_send()
    for h in range(2):
        zpre(zl, h).wait_send()
    for d in range(4):
        swap(d).wait_send()
    for piece in give[0] + give[1]:
        piece.wait_send()

    @pl.when(other)
    def _():
        first(0).wait_send()
        tok_copy(0).wait_send()


def local(tokens, norm_gain, filters, mixing):
    rows, width = tokens.shape
    bf16, f32 = jnp.bfloat16, jnp.float32
    dma = pltpu.SemaphoreType.DMA
    vmem = pl.BlockSpec(memory_space=pltpu.VMEM)
    result = pl.BlockSpec(memory_space=pl.ANY)
    return pl.pallas_call(
        kernel,
        out_shape=jax.ShapeDtypeStruct((rows, width), bf16),
        in_specs=[vmem] * 4,
        out_specs=result,
        scratch_shapes=[
            pltpu.VMEM((rows, width), bf16),
            pltpu.VMEM((8, BLK), bf16),
            pltpu.VMEM((NB, 8, BLK), bf16),
            pltpu.VMEM((HALF * BLK, (NB + PAD) * BLK), bf16),
            pltpu.VMEM((HALF * BLK, BLK), f32),
            pltpu.VMEM((4, 16, BLK, GRP), bf16),
            pltpu.VMEM((HALF * BLK, GRP), f32),
            pltpu.VMEM((8 * BLK, HALF * GRP), bf16),
            pltpu.VMEM((HALF, 16, 16, width), bf16),
            pltpu.VMEM((4, BLK, width), bf16),
            pltpu.VMEM((4, BLK, width), bf16),
            pltpu.VMEM((4, BLK, width), f32),
            pltpu.VMEM((4, BLK, width), bf16),
            pltpu.VMEM((4, 3, PIECE, width), bf16),
            pltpu.VMEM((4, PIECE, width), bf16),
            pltpu.VMEM((4, PIECE, width), bf16),
            dma((2,)), dma((2,)), dma((4,)), dma((4,)), dma((2,)), dma((4,)), dma((4,)),
            dma((16,)), dma((16,)), dma((2,)), dma((2,)), dma((16,)), dma((16,)),
            dma((3,)), dma((3,)), dma((4, 4)), dma((4, 4)), dma((1,)), dma((4,)), dma((4,)),
            dma((4, 3)), dma((4, 3)), dma((4,)), dma((4,)), dma((1,)),
        ],
        compiler_params=pltpu.CompilerParams(
            collective_id=0, has_side_effects=True, vmem_limit_bytes=56 * 1024 * 1024
        ),
    )(tokens, norm_gain.reshape(1, width), filters, mixing)


def solution(mesh):
    grid = Mesh(mesh.devices.reshape(4, 4, 4, 2, 2), AXES)
    seq = ("x", "zh", "y")
    in_specs = (P(("zl", "q") + seq, None), P(), P(None, seq), P(None, seq, None))
    out_specs = P(("zl", "q") + seq, None)
    return jax.shard_map(local, mesh=grid, in_specs=in_specs, out_specs=out_specs, check_vma=False)
```
